32 devices in a mesh: parts: 2 (over y), ctx: 4 (over z), width: 2 (over x), sub: 2 (over core).
Axes of the slice: x: 2, y: 2, z: 4, core: 2. Of those that a mesh axis runs over, the one named last changes fastest.
Arguments:
- tokens: bfloat16 [4096, 8192], P(('parts', 'ctx'), 'width'), parts along dimension 0, may hold values from -4 to 4
- norm_gain: float32 [8192], P('width'), may hold values from 0.25 to 1.75
- in_weight: bfloat16 [3, 8192, 2, 2048], P(None, 'width', 'sub', 'ctx'), may hold values from -0.09375 to 0.09375
- short_taps: float32 [3, 3, 2, 2048], P(None, None, 'sub', 'width'), may hold values from -3 to 3
- long_taps: float32 [128, 2, 2048], P(None, 'sub', 'width'), may hold values from -0.5 to 0.5
Outputs:
- output: bfloat16 [4096, 2, 2048], P(('parts', 'ctx'), 'sub', 'width'), parts along dimension 0
The draws below stay inside these ranges and needn't reach their ends.
There are 2 independent parts, one for each index of `parts`. The reference program is written for one: setup_inputs(seed, part) draws one part's arguments, and reference() takes and returns one part's arrays. A program takes and returns all parts, laid end to end along the dimension named above; an argument that names none is the same for every part. Nothing has to cross between parts.
All inputs are finite; a program needn't handle non-finite values.
Results may differ from the reference program's by a relative error of at most 0.025.
Values may be sent and summed in bfloat16 or wider, within the bound.
No kernel may reach another device: no remote copies, remote signals or barrier semaphores. Data moves between devices by JAX's collectives and lax.ppermute only.
A program may use at most 192 MiB of HBM per device.

```python
import jax
import jax.numpy as jnp
from jax import lax

D = 8192
KLEN = 128
C = 4096
TOK_DEV = 512
TOKENS = 2048
N_SUB = 2


def draw_tokens(key, part):
    key_base, key_rows, key_cols = jax.random.split(key, 3)
    row_scale = 10.0 ** (-jax.random.uniform(key_rows, (TOKENS, 1), jnp.float32))
    channel_trend = 3.0 ** (jnp.arange(D, dtype=jnp.float32) / D - 1.0)
    col_scale = 10.0 ** (-jax.random.uniform(key_cols, (D,), jnp.float32)) * channel_trend
    base_draw = jnp.clip(jax.random.normal(key_base, (TOKENS, D), jnp.float32), -4.0, 4.0)
    return jnp.clip(base_draw * row_scale * col_scale[None, :], -4.0, 4.0).astype(jnp.bfloat16)


def strengthened(entries, stream_key, source, target, blocks, factor):
    owner, partner = [(jnp.arange(entries.shape[position]) // (entries.shape[position] // blocks)).reshape([-1 if axis == position else 1 for axis in range(entries.ndim)]) for position in (source, target)]
    chosen = jax.random.permutation(stream_key, blocks)[partner]
    strong = (owner == chosen) | (owner == (partner + blocks // 2) % blocks)
    return jnp.where(strong, factor * entries, entries)


def levels(stream_key, extent, cuts, low, largest):
    loudness = 1.0
    for position, parts in cuts:
        heights = jax.random.uniform(jax.random.fold_in(jax.random.fold_in(stream_key, 6), position), (parts,), jnp.float32, low / len(cuts), largest / len(cuts))
        loudness = loudness * jnp.repeat(jnp.exp(heights), extent[position] // parts).reshape((-1,) + (1,) * (len(extent) - 1 - position))
    return loudness


def scatter_about(own_key, extent, deviation, bound, cuts=(), kind=jnp.bfloat16):
    values = jax.random.normal(own_key, extent, jnp.float32) * deviation
    if len(cuts) > 0:
        values = levels(own_key, extent, cuts, -0.22, 0.18) * values
    return jnp.clip(values, min=-bound, max=bound).astype(kind)


def noise_with(own_key, dims, spread, limit, pieces, heavy, kind=jnp.bfloat16):
    entries = spread * jax.random.normal(own_key, dims, jnp.float32)
    if pieces:
        entries = entries * levels(own_key, dims, pieces, -0.22, 0.18)
    return jnp.clip(strengthened(entries, jax.random.fold_in(own_key, 3), *heavy), -limit, limit).astype(kind)


def setup_inputs(seed: int = 0, part: int = 0) -> dict:
    seeds = jax.random.split(jax.random.key(seed), 6)
    own_keys = jax.random.split(jax.random.fold_in(seeds[5], part), 6)
    return {
        "tokens": draw_tokens(jax.random.fold_in(jax.random.fold_in(seeds[5], part), 71), part),
        "norm_gain": jnp.clip(1.0 + 0.15 * jax.random.normal(seeds[1], (D,), jnp.float32), 0.25, 1.75),
        "in_weight": noise_with(seeds[2], (3, D, N_SUB, C // N_SUB), D ** -0.5, 0.09375, ((1, 2), (2, 2), (3, 4)), (1, 3, 4, 2.0)),
        "short_taps": scatter_about(seeds[3], (3, 3, N_SUB, C // N_SUB), 0.6, 3.0, ((2, 2), (3, 2)), jnp.float32),
        "long_taps": scatter_about(seeds[4], (KLEN, N_SUB, C // N_SUB), KLEN ** -0.5, 0.5, ((1, 2), (2, 2)), jnp.float32),
    }


epsilon = 1e-05

def short_filter(padded, tap_set):
    widened = padded.astype(jnp.float32)
    length_out = padded.shape[0] - 2
    return tap_set[0] * widened[2:] + tap_set[1] * widened[1:length_out + 1] + tap_set[2] * widened[:length_out]

def reference(tokens, norm_gain, in_weight, short_taps, long_taps):
    weights = in_weight.reshape(3, D, C)

    def project_block(block):
        values = block.astype(jnp.float32)
        power = lax.optimization_barrier(jnp.sum(values * values, axis=1))
        scaled = (values * lax.rsqrt(power / D + epsilon)[:, None] * norm_gain[None, :]).astype(jnp.bfloat16)
        streams = [jnp.dot(scaled, weights[stream], preferred_element_type=jnp.float32) for stream in range(3)]
        return jnp.stack(streams, axis=1).astype(jnp.bfloat16)
    blocks = tokens.reshape(TOKENS // TOK_DEV, TOK_DEV, D)
    projected = lax.map(project_block, blocks).reshape(TOKENS, 3, C)
    tap_set = short_taps.reshape(3, 3, C)
    padded = jnp.concatenate([jnp.zeros((2, 3, C), jnp.bfloat16), projected], axis=0)
    filtered = short_filter(padded, tap_set)
    gated = (filtered[:, 1] * filtered[:, 2]).astype(jnp.bfloat16)
    extended = jnp.concatenate([jnp.zeros((KLEN - 1, C), jnp.bfloat16), gated], axis=0).astype(jnp.float32)
    long_filter = long_taps.reshape(KLEN, C)

    def add_tap(index, total):
        window = lax.dynamic_slice_in_dim(extended, (KLEN - 1 - index).astype(jnp.int32), TOKENS, 0)
        return total + long_filter[index] * window
    convolved = lax.fori_loop(jnp.int32(0), jnp.int32(KLEN), add_tap, jnp.zeros((TOKENS, C), jnp.float32))
    output = (filtered[:, 0] * convolved).astype(jnp.bfloat16)
    return output.reshape(TOKENS, N_SUB, C // N_SUB)
```

```python
import functools

import jax
import jax.numpy as jnp
import numpy as np
from jax import lax
from jax.experimental import pallas as pl
from jax.experimental.pallas import tpu as pltpu
from jax.sharding import PartitionSpec as P

EPSILON = 1e-05
HALO = 144
FFT = 256
STEP = 128
BF16 = jnp.bfloat16
F32 = jnp.float32


def split(matrix):
    high = np.asarray(matrix, np.float32).astype(jnp.bfloat16)
    low = (np.asarray(matrix, np.float32) - high.astype(np.float32)).astype(jnp.bfloat16)
    return high, low


def transforms():
    half = FFT // 2
    n = np.arange(FFT)
    k = np.arange(half)
    angle = 2.0 * np.pi * np.outer(k, n) / FFT
    real, imag = np.cos(angle), -np.sin(angle)
    imag[0] = np.cos(np.pi * n)
    forward = np.concatenate([real, imag], axis=0)
    weight = np.full((half,), 2.0)
    weight[0] = 1.0
    back_real = (weight[:, None] * np.cos(angle)).T / FFT
    back_imag = (-2.0 * np.sin(angle)).T / FFT
    back_imag[:, 0] = np.cos(np.pi * n) / FFT
    inverse = np.concatenate([back_real, back_imag], axis=1)[FFT - STEP :]
    return forward, inverse


def project_kernel(count, *refs):
    scalars, refs = refs[0], refs[1:]
    parts, weights, out = refs[:count], refs[count : 2 * count], refs[2 * count]
    total = jnp.dot(parts[0][...], weights[0][0], preferred_element_type=F32)
    for part, weight in zip(parts[1:], weights[1:]):
        total = total + jnp.dot(part[...], weight[0], preferred_element_type=F32)
    out[0] = total.astype(BF16)


def project(parts, weight, sub, column, kept):
    count = len(parts)
    rows, depth = parts[0].shape
    streams = weight.shape[0]
    if kept % 128 and kept != weight.shape[2]:
        weight = lax.dynamic_slice_in_dim(weight, column * kept, kept, 2)
        column = column * 0
    scalars = jnp.stack([sub, column]).astype(jnp.int32)

    def weight_spec(offset):
        return pl.BlockSpec(
            (1, depth, kept), lambda i, s: (i, lax.rem(s[0] + offset, count), s[1])
        )

    return pl.pallas_call(
        functools.partial(project_kernel, count),
        out_shape=jax.ShapeDtypeStruct((streams, rows, kept), BF16),
        grid_spec=pltpu.PrefetchScalarGridSpec(
            num_scalar_prefetch=1,
            grid=(streams,),
            in_specs=[pl.BlockSpec((rows, depth), lambda i, s: (0, 0)) for _ in parts]
            + [weight_spec(o) for o in range(count)],
            out_specs=pl.BlockSpec((1, rows, kept), lambda i, s: (i, 0, 0)),
        ),
        compiler_params=pltpu.CompilerParams(
            dimension_semantics=("arbitrary",), vmem_limit_bytes=24 << 20
        ),
        cost_estimate=pl.CostEstimate(
            flops=2 * rows * depth * count * streams * kept,
            bytes_accessed=2 * (rows * depth * count + depth * count * streams * kept + rows * streams * kept),
            transcendentals=0,
        ),
        name="project",
    )(scalars, *parts, *[weight] * count)


def filter_kernel(plan, terms, rows, *refs):
    flag, refs = refs[0], refs[1:]
    pieces = []
    for _ in plan:
        pieces.append(refs[:terms])
        refs = refs[terms:]
    near, far, short, spec_a, spec_b, spec_c, fh, fl, gh, gl, out, held, query, gated = refs
    tile = 64
    at = 0
    for (first, count, scale, scale_first, masked), sources in zip(plan, pieces):
        scales = (near, far)[scale]
        for low in range(0, count, tile):
            size = min(tile, count - low)
            factor = scales[0, scale_first + low : scale_first + low + size, :]
            if masked:
                factor = factor * flag[1].astype(F32)
            for stream in range(3):
                total = sources[0][stream, first + low : first + low + size, :].astype(F32)
                for source in sources[1:]:
                    total = total + source[stream, first + low : first + low + size, :].astype(F32)
                value = (total * factor).astype(BF16).astype(F32)
                held[stream, at + low : at + low + size, :] = value
        at += count

    def short_filter(stream, row, size):
        taps = [short[j, stream][None, :] for j in range(3)]
        return sum(taps[j] * held[stream, row - j : row - j + size, :] for j in range(3))

    lead = HALO - STEP
    for low in range(0, STEP + rows, tile):
        value = short_filter(1, lead + low, tile) * short_filter(2, lead + low, tile)
        gated[low : low + tile, :] = value.astype(BF16)
    for low in range(0, rows, tile):
        query[low : low + tile, :] = short_filter(0, HALO + low, tile)
    half = FFT // 2
    starts = [min(s, rows - STEP) for s in range(0, rows, STEP)]
    for start in starts:
        window = gated[start : start + FFT, :]
        spectrum = jnp.dot(fh[...], window, preferred_element_type=F32)
        spectrum = spectrum + jnp.dot(fl[...], window, preferred_element_type=F32)
        upper, lower = spectrum[:half], spectrum[half:]
        product = jnp.concatenate(
            [upper * spec_a[...] - lower * spec_b[...], upper * spec_b[...] + lower * spec_c[...]], axis=0
        )
        high = product.astype(BF16)
        rest = (product - high.astype(F32)).astype(BF16)
        result = jnp.dot(gh[...], high, preferred_element_type=F32)
        result = result + jnp.dot(gh[...], rest, preferred_element_type=F32)
        result = result + jnp.dot(gl[...], high, preferred_element_type=F32)
        out[start : start + STEP, :] = (result * query[start : start + STEP, :]).astype(BF16)


def filter_rows(plan, pieces, scales, index, follows, short, spectra, matrices, rows):
    terms = len(pieces[0])
    streams, _, kept = pieces[0][0].shape
    before = lax.rem(index + scales.shape[0] - 1, scales.shape[0])
    scalars = jnp.stack([index, follows, before]).astype(jnp.int32)
    arrays = [array for piece in pieces for array in piece]
    whole = lambda array: pl.BlockSpec(array.shape, lambda i, s, n=array.ndim: (0,) * n)
    scale_block = (1,) + scales.shape[1:]
    reach = HALO + rows
    constants = [short, *spectra, *matrices]
    return pl.pallas_call(
        functools.partial(filter_kernel, plan, terms, rows),
        out_shape=jax.ShapeDtypeStruct((rows, kept), BF16),
        grid_spec=pltpu.PrefetchScalarGridSpec(
            num_scalar_prefetch=1,
            grid=(1,),
            in_specs=[whole(a) for a in arrays]
            + [
                pl.BlockSpec(scale_block, lambda i, s: (s[0], 0, 0)),
                pl.BlockSpec(scale_block, lambda i, s: (s[2], 0, 0)),
            ]
            + [whole(c) for c in constants],
            out_specs=pl.BlockSpec((rows, kept), lambda i, s: (0, 0)),
            scratch_shapes=[
                pltpu.VMEM((streams, reach, kept), F32),
                pltpu.VMEM((rows, kept), F32),
                pltpu.VMEM((STEP + rows, kept), BF16),
            ],
        ),
        compiler_params=pltpu.CompilerParams(vmem_limit_bytes=24 << 20),
        cost_estimate=pl.CostEstimate(
            flops=2 * 5 * FFT * FFT * kept * (rows // STEP + 1),
            bytes_accessed=sum(a.size * 2 for a in arrays) + 2 * rows * kept,
            transcendentals=0,
        ),
        name="filter",
    )(scalars, *arrays, scales, scales, *constants)


def shards(tokens, norm_gain, in_weight, short_taps, long_taps):
    steps, across, cores = (lax.axis_size(a) for a in ("ctx", "width", "sub"))
    z, x, sub = (lax.axis_index(a) for a in ("ctx", "width", "sub"))
    rows, features = tokens.shape
    weight = in_weight[:, :, 0, :]
    panel = weight.shape[2]
    kept = panel // across
    group = steps // across
    owner = z // group
    depth = features // cores
    mid, small, late = rows // 2, 48, 192

    power = jnp.sum(tokens.astype(F32) ** 2, axis=1)

    def scaled_part(first, count, offset):
        column = lax.rem(sub + offset, cores) * depth
        block = lax.dynamic_slice(tokens, (first, column), (count, depth)).astype(F32)
        gain = lax.dynamic_slice(norm_gain, (column,), (depth,))
        return (block * gain[None, :]).astype(BF16)

    ring = [(i, (i + 1) % steps) for i in range(steps)]
    forward = lambda block: lax.ppermute(block, "ctx", ring)

    def all_parts(block):
        swaps = [[((c + o) % cores, c) for c in range(cores)] for o in range(1, cores)]
        return [block] + [lax.ppermute(block, "sub", swap) for swap in swaps]

    def partials(parts):
        received = []
        for w in range(1, across):
            block = project(parts, weight, sub, lax.rem(x + w, across), kept)
            received.append(lax.ppermute(block, "width", [(i, (i + w) % across) for i in range(across)]))
        return [project(parts, weight, sub, x, kept)] + received

    halves = [(mid, rows - mid), (0, mid)]
    last = [(mid, rows - mid), (small, mid - small), (0, small)]
    moving = [scaled_part(first, count, 0) for first, count in halves]
    table = {}
    for (first, count), block in zip(halves, moving):
        table[0, first] = partials([block] + [scaled_part(first, count, o) for o in range(1, cores)])
    gathered = lax.all_gather(power, ("ctx", "width"), axis=0).reshape(steps, across, rows).sum(axis=1)
    scales = lax.rsqrt(gathered / (features * across) + EPSILON)[:, :, None]

    for step in range(1, steps):
        if step < steps - 1:
            moving = [forward(block) for block in moving]
            spans = halves
        else:
            upper, lower = moving
            moving = [forward(upper), forward(lower[small:]), forward(lower[:small])]
            spans = last
        for (first, count), block in zip(spans, moving):
            table[step, first] = partials(all_parts(block))

    def taps_of(taps):
        offset = lambda v: lax.rem(z, group) * panel + v * kept
        cut = lambda v: lax.dynamic_slice_in_dim(taps, offset(v), kept, taps.ndim - 1)
        result = cut(x)
        for w in range(1, across):
            other = lax.ppermute(cut(lax.rem(x + w, across)), "width", [(i, (i + w) % across) for i in range(across)])
            result = jnp.where(lax.rem(owner + w, across) == x, other, result)
        return result

    short = taps_of(short_taps[:, :, 0, :])
    long = taps_of(long_taps[:, 0, :])
    forward_dft, inverse_dft = transforms()
    spectrum = jnp.dot(
        jnp.asarray(forward_dft[:, : long.shape[0]], F32), long, precision=lax.Precision.HIGHEST
    )
    upper, lower = spectrum[: FFT // 2], spectrum[FFT // 2 :]
    first_row = (jnp.arange(FFT // 2) == 0)[:, None]
    spectra = [upper, jnp.where(first_row, 0.0, lower), jnp.where(first_row, lower, upper)]
    matrices = [jnp.asarray(m) for pair in (split(forward_dft), split(inverse_dft)) for m in pair]

    def unit(step, plan, pieces, count):
        index = lax.rem(z - step + steps, steps)
        return filter_rows(plan, pieces, scales, index, jnp.where(index > 0, 1, 0), short, spectra, matrices, count)

    tail = rows - mid
    before = (tail - HALO, HALO, 1, rows - HALO, True)
    done = []
    for step in range(steps - 1):
        plan = (before, (0, mid, 0, 0, False), (0, tail, 0, mid, False))
        pieces = [table[step + 1, mid], table[step, 0], table[step, mid]]
        done.append(unit(step, plan, pieces, rows))
    step = steps - 1
    early = unit(
        step,
        ((late - HALO - small, mid - (late - HALO), 0, late - HALO, False), (0, tail, 0, mid, False)),
        [table[step, small], table[step, mid]],
        rows - late,
    )
    begin = unit(
        step,
        (before, (0, small, 0, 0, False), (0, late - small, 0, small, False)),
        [table[0, mid], table[step, 0], table[step, small]],
        late,
    )

    part = lax.rem(x - owner + across, across)

    def chosen(k, cut):
        options = [cut((k + group * w) % steps) for w in range(across)]
        result = options[0]
        for w in range(1, across):
            result = jnp.where(part == w, options[w], result)
        return result

    def returned(k, block):
        pairs = []
        for c in range(steps):
            for v in range(across):
                w = (v - c // group) % across
                target = (c - k - group * w) % steps
                pairs.append((c * across + v, target * across + c // group))
        return lax.ppermute(block, ("ctx", "width"), pairs)

    def place(output, k, block, first):
        source = group * x + lax.rem(z + k, group)
        w = lax.rem((source - z - k + 2 * steps) // group, across)
        column = lax.rem(source, group) * panel + lax.rem(x + w, across) * kept
        return lax.dynamic_update_slice(output, block, (first, column))

    output = jnp.zeros((rows, panel * group), BF16)
    rounds = [k for k in range(steps) if any((k + group * w) % steps == steps - 1 for w in range(across))]
    for k in range(steps):
        if k not in rounds:
            output = place(output, k, returned(k, chosen(k, lambda j: done[j])), 0)
    for k in rounds:
        block = chosen(k, lambda j: early if j == steps - 1 else done[j][late:])
        output = place(output, k, returned(k, block), late)
    for k in rounds:
        block = chosen(k, lambda j: begin if j == steps - 1 else done[j][:late])
        output = place(output, k, returned(k, block), 0)
    return output[:, None, :]


def solution(mesh):
    placed = (
        P(("parts", "ctx"), "width"),
        P("width"),
        P(None, "width", "sub", "ctx"),
        P(None, None, "sub", "width"),
        P(None, "sub", "width"),
    )
    return jax.shard_map(
        shards,
        mesh=mesh,
        in_specs=placed,
        out_specs=P(("parts", "ctx"), "sub", "width"),
        check_vma=False,
    )
```

```python
import functools

import jax
import jax.numpy as jnp
import numpy as np
from jax import lax
from jax.experimental import pallas as pl
from jax.experimental.pallas import tpu as pltpu
from jax.sharding import PartitionSpec as P

EPSILON = 1e-05
HALO = 144
FFT = 256
STEP = 128
EXTRA = 8
BF16 = jnp.bfloat16
F32 = jnp.float32


def repeat(count, unrolled, body):
    if unrolled:
        for i in range(count):
            body(i)
    else:
        pl.loop(0, count)(body)


def at_multiple(value, multiple):
    return value if isinstance(value, int) else pl.multiple_of(value, multiple)


def split(matrix):
    high = np.asarray(matrix, np.float32).astype(jnp.bfloat16)
    low = (np.asarray(matrix, np.float32) - high.astype(np.float32)).astype(jnp.bfloat16)
    return high, low


def transforms():
    half = FFT // 2
    n = np.arange(FFT)
    k = np.arange(half)
    angle = 2.0 * np.pi * np.outer(k, n) / FFT
    real, imag = np.cos(angle), -np.sin(angle)
    imag[0] = np.cos(np.pi * n)
    forward = np.concatenate([real, imag], axis=0)
    weight = np.full((half,), 2.0)
    weight[0] = 1.0
    back_real = (weight[:, None] * np.cos(angle)).T / FFT
    back_imag = (-2.0 * np.sin(angle)).T / FFT
    back_imag[:, 0] = np.cos(np.pi * n) / FFT
    inverse = np.concatenate([back_real, back_imag], axis=1)[FFT - STEP :]
    return forward, inverse


def project(parts, rows, weight, places, column, kept):
    depth = parts[0].shape[1]
    streams = weight.shape[0]
    count = len(parts)

    narrow = weight.shape[2] == kept

    def body(places, *refs):
        blocks, weight, out = refs[:count], refs[count], refs[count + 1]
        columns = slice(None) if narrow else pl.ds(pl.multiple_of(places[column] * kept, kept), kept)

        def one(stream):
            total = None
            for offset, block in enumerate(blocks):
                row = pl.multiple_of(lax.rem(places[0] + offset, count) * depth, depth)
                term = jnp.dot(
                    block[:rows, :], weight[stream, pl.ds(row, depth), columns], preferred_element_type=F32
                )
                total = term if total is None else total + term
            out[stream] = total.astype(BF16)

        repeat(streams, rows < 256, one)

    whole = pl.BlockSpec(memory_space=pltpu.VMEM)
    return pl.pallas_call(
        body,
        out_shape=jax.ShapeDtypeStruct((streams, rows, kept), BF16),
        in_specs=[pl.BlockSpec(memory_space=pltpu.SMEM)] + [whole] * (count + 1),
        out_specs=whole,
        compiler_params=pltpu.CompilerParams(vmem_limit_bytes=12 << 20),
        cost_estimate=pl.CostEstimate(flops=1 << 20, bytes_accessed=1 << 16, transcendentals=0),
        name="project",
    )(places, *parts, pltpu.with_memory_space_constraint(weight, pltpu.VMEM))


def filter_kernel(plan, terms, rows, flag, places, *refs):
    pieces = []
    for _ in plan:
        pieces.append(refs[:terms])
        refs = refs[terms:]
    near, far, short, spec_a, spec_b, spec_c, fh, fl, gh, gl, out, held, query, gated, spread = refs
    tile = 64
    kept = out.shape[1]
    extent = spread.shape[1]
    for which, scale in enumerate((near, far)):
        row = scale[0:1, :extent].astype(F32) + scale[1:2, :extent].astype(F32) + scale[2:3, :extent].astype(F32)
        for low in range(0, extent, 128):
            spread[which, low : low + 128, :] = jnp.broadcast_to(row[:, low : low + 128], (128, 128)).T
    at = 0
    for (first, count, scale, scale_first, masked), sources in zip(plan, pieces):
        for low in range(0, count, tile):
            size = min(tile, count - low)
            factor = spread[scale, scale_first + low : scale_first + low + size, :]
            if masked:
                factor = factor * places[flag].astype(F32)
            factor = jnp.concatenate([factor] * (kept // 128), axis=1) if kept % 128 == 0 else factor[:, :kept]
            for stream in range(3):
                total = sources[0][stream, first + low : first + low + size, :].astype(F32)
                for source in sources[1:]:
                    total = total + source[stream, first + low : first + low + size, :].astype(F32)
                value = (total * factor).astype(BF16).astype(F32)
                held[stream, at + low : at + low + size, :] = value
        at += count

    def short_filter(stream, row):
        window = held[stream, pl.ds(at_multiple(row - 8, 8), tile + 8), :]
        return sum(short[j, stream][None, :] * window[8 - j : 8 - j + tile] for j in range(3))

    lead = HALO - STEP

    def gate(i):
        low = at_multiple(i * tile, tile)
        value = short_filter(1, lead + low) * short_filter(2, lead + low)
        gated[pl.ds(low, tile), :] = value.astype(BF16)

    def ask(i):
        low = at_multiple(i * tile, tile)
        query[pl.ds(low, tile), :] = short_filter(0, HALO + low)

    half = FFT // 2

    def convolve(i):
        start = min(i * STEP, rows - STEP) if isinstance(i, int) else jnp.minimum(i * STEP, rows - STEP)
        start = at_multiple(start, tile)
        window = gated[pl.ds(start, FFT), :]
        spectrum = jnp.dot(fh[...], window, preferred_element_type=F32)
        spectrum = spectrum + jnp.dot(fl[...], window, preferred_element_type=F32)
        upper, lower = spectrum[:half], spectrum[half:]
        product = jnp.concatenate(
            [upper * spec_a[...] - lower * spec_b[...], upper * spec_b[...] + lower * spec_c[...]], axis=0
        )
        high = product.astype(BF16)
        rest = (product - high.astype(F32)).astype(BF16)
        result = jnp.dot(gh[...], high, preferred_element_type=F32)
        result = result + jnp.dot(gh[...], rest, preferred_element_type=F32)
        result = result + jnp.dot(gl[...], high, preferred_element_type=F32)
        out[pl.ds(start, STEP), :] = (result * query[pl.ds(start, STEP), :]).astype(BF16)

    unrolled = rows < 512
    repeat((STEP + rows) // tile, unrolled, gate)
    repeat(rows // tile, unrolled, ask)
    repeat(-(-rows // STEP), unrolled, convolve)


def filter_rows(plan, pieces, scales, flag, places, short, spectra, matrices, rows):
    terms = len(pieces[0])
    streams, _, kept = pieces[0][0].shape
    extent = scales[0].shape[1]
    arrays = [array for piece in pieces for array in piece]
    constants = [*scales, short, *spectra, *matrices]
    whole = pl.BlockSpec(memory_space=pltpu.VMEM)
    return pl.pallas_call(
        functools.partial(filter_kernel, plan, terms, rows, flag),
        out_shape=jax.ShapeDtypeStruct((rows, kept), BF16),
        in_specs=[pl.BlockSpec(memory_space=pltpu.SMEM)] + [whole] * (len(arrays) + len(constants)),
        out_specs=whole,
        scratch_shapes=[
            pltpu.VMEM((streams, HALO + rows, kept), F32),
            pltpu.VMEM((rows, kept), F32),
            pltpu.VMEM((STEP + rows, kept), BF16),
            pltpu.VMEM((2, extent, 128), F32),
        ],
        compiler_params=pltpu.CompilerParams(vmem_limit_bytes=12 << 20),
        cost_estimate=pl.CostEstimate(flops=1 << 20, bytes_accessed=1 << 16, transcendentals=0),
        name="filter",
    )(places, *arrays, *constants)


def shards(tokens, norm_gain, in_weight, short_taps, long_taps):
    steps, across, cores = (lax.axis_size(a) for a in ("ctx", "width", "sub"))
    z, x, sub = (lax.axis_index(a) for a in ("ctx", "width", "sub"))
    rows, features = tokens.shape
    panel = in_weight.shape[3]
    kept = panel // across
    group = steps // across
    owner = z // group
    depth = features // cores
    mid, small, late = rows // 2, 48, 192

    kinds = range(across)
    places = [sub] + [lax.rem(x + w, across) for w in kinds]
    flag_at = len(places)
    places += [jnp.where(z == k % steps, 0, 1) for k in range(steps)]
    starts = [lax.rem(sub + o, cores) * depth for o in range(cores)]
    part = lax.rem(x - owner + across, across)
    mine = [part == w for w in kinds]
    tap_first = [lax.rem(z, group) * panel + lax.rem(x + w, across) * kept for w in kinds]
    targets = []
    for k in range(steps):
        source = group * x + lax.rem(z + k, group)
        w = lax.rem((source - z - k + 2 * steps) // group, across)
        targets.append(lax.rem(source, group) * panel + lax.rem(x + w, across) * kept)
    places = jnp.stack(places).astype(jnp.int32)
    if kept % 128 == 0:
        targets = jnp.stack(targets).astype(jnp.int32)
    tokens, places, starts, mine, tap_first, targets = lax.optimization_barrier(
        (tokens, places, starts, mine, tap_first, targets)
    )

    def scaled_part(source, first, count, offset):
        block = lax.dynamic_slice(source, (first, starts[offset]), (count, depth)).astype(F32)
        gain = lax.dynamic_slice(norm_gain, (starts[offset],), (depth,))
        return (block * gain[None, :]).astype(BF16)

    ring = [(i, (i + 1) % steps) for i in range(steps)]
    forward = lambda block: lax.ppermute(block, "ctx", ring)

    def sideways(block, w):
        return lax.ppermute(block, "width", [(i, (i + w) % across) for i in range(across)])

    def all_parts(block):
        swaps = [[((c + o) % cores, c) for c in range(cores)] for o in range(1, cores)]
        return [block] + [lax.ppermute(block, "sub", swap) for swap in swaps]

    weight = in_weight[:, :, 0, :]

    def partial(parts, count, w):
        if kept % 128:
            first = lax.rem(x + w, across) * kept
            narrow = lax.dynamic_slice_in_dim(weight, first, kept, 2)
            return project(parts, count, narrow, places, 1, kept)
        return project(parts, count, weight, places, 1 + w, kept)

    def partials(parts, count):
        sent = [partial(parts, count, w) for w in range(1, across)]
        received = [sideways(block, w + 1) for w, block in enumerate(sent)]
        kept_block = partial(parts, count, 0)
        return [kept_block] + sent, [kept_block] + received

    halves = [(mid, rows - mid), (0, mid)]
    last = [(mid, rows - mid), (small, mid - small), (0, small)]
    first, count = halves[0]
    upper = scaled_part(tokens, first, count, 0)
    source, upper = lax.optimization_barrier((tokens, upper))
    power = jnp.sum(source.astype(F32) ** 2, axis=1)
    whole_power = power
    for w in range(1, across):
        whole_power = whole_power + sideways(power, w)
    scale = lax.rsqrt(whole_power / (features * across) + EPSILON)
    terms = [lax.reduce_precision(scale, 8, 7)]
    terms.append(lax.reduce_precision(scale - terms[0], 8, 7))
    terms.append(scale - terms[0] - terms[1])
    extra = jnp.pad(jnp.stack(terms), ((0, EXTRA - 3), (0, depth - rows))).astype(BF16)
    first, count = halves[1]
    lower = jnp.concatenate([scaled_part(source, first, count, 0), extra], axis=0)
    scales = [extra[:, :rows]]

    def taps_of(taps):
        cut = lambda w: lax.dynamic_slice_in_dim(taps, tap_first[w], kept, taps.ndim - 1)
        result = cut(0)
        for w in range(1, across):
            other = sideways(cut(w), w)
            result = jnp.where(mine[w], other, result)
        return result

    short = taps_of(short_taps[:, :, 0, :])
    long = taps_of(long_taps[:, 0, :])
    forward_dft, inverse_dft = transforms()
    spectrum = jnp.dot(
        jnp.asarray(forward_dft[:, : long.shape[0]], F32), long, precision=lax.Precision.HIGHEST
    )
    real, imag = spectrum[: FFT // 2], spectrum[FFT // 2 :]
    first_row = (jnp.arange(FFT // 2) == 0)[:, None]
    spectra = [real, jnp.where(first_row, 0.0, imag), jnp.where(first_row, imag, real)]
    matrices = [jnp.asarray(m) for pair in (split(forward_dft), split(inverse_dft)) for m in pair]

    def unit(step, plan, pieces, count):
        near_far = (scales[step], scales[(step + 1) % steps])
        return filter_rows(plan, pieces, near_far, flag_at + step, places, short, spectra, matrices, count)

    tail = rows - mid
    before = (tail - HALO, HALO, 1, rows - HALO, True)

    def whole_unit(step):
        plan = (before, (0, mid, 0, 0, False), (0, tail, 0, mid, False))
        return unit(step, plan, [table[step + 1, mid], table[step, 0], table[step, mid]], rows)

    table, done = {}, {}
    received, ready = [], set()
    held = {"filters": (short, spectra)}
    waiting = []

    def multiply(key, parts, count):
        local, table[key] = partials(parts, count)
        held["local", key] = local
        received.append(key)

    def arrived(block):
        coming = [key for key in received[:-1] if key not in ready]
        names = list(held)
        pack = (block, [held[n] for n in names], [table[key] for key in coming])
        block, kept_back, blocks = lax.optimization_barrier(pack)
        for key, value in zip(coming, blocks):
            table[key] = value
            ready.add(key)
        for name, value in zip(names, kept_back):
            if name[0] == "unit":
                done[name[1]] = value
        held.clear()
        return block

    def filter_ready():
        for step in range(steps - 1):
            if step not in done and {(step + 1, mid), (step, 0), (step, mid)} <= ready:
                done[step] = whole_unit(step)
                held["unit", step] = done[step]

    for (first, count), block in zip(halves, [upper, lower]):
        own = [block] + [scaled_part(source, first, count, o) for o in range(1, cores)]
        multiply((0, first), own, count)

    moving = [upper, lower]
    for step in range(1, steps):
        if step < steps - 1:
            spans = halves
            moving = [forward(block) for block in moving]
        else:
            spans = last
            upper, lower = moving
            moving = [forward(upper), forward(lower[small:]), forward(lower[:small])]
        for i, (first, count) in enumerate(spans):
            moving[i] = arrived(moving[i])
            if i == 1:
                scales.append(moving[1][-EXTRA:, :rows])
            waiting.append(((step, first), all_parts(moving[i]), count))
            if len(waiting) > 1:
                multiply(*waiting.pop(0))
            filter_ready()
    while waiting:
        multiply(*waiting.pop(0))
    for step in range(steps - 1):
        if step not in done:
            done[step] = whole_unit(step)
    step = steps - 1
    early = unit(
        step,
        ((late - HALO - small, mid - (late - HALO), 0, late - HALO, False), (0, tail, 0, mid, False)),
        [table[step, small], table[step, mid]],
        rows - late,
    )
    begin = unit(
        step,
        (before, (0, small, 0, 0, False), (0, late - small, 0, small, False)),
        [table[0, mid], table[step, 0], table[step, small]],
        late,
    )

    def chosen(k, cut):
        options = [cut((k + group * w) % steps) for w in kinds]
        result = options[0]
        for w in range(1, across):
            result = jnp.where(mine[w], options[w], result)
        return result

    def returned(k, block):
        pairs = []
        for c in range(steps):
            for v in kinds:
                w = (v - c // group) % across
                target = (c - k - group * w) % steps
                pairs.append((c * across + v, target * across + c // group))
        return lax.ppermute(block, ("ctx", "width"), pairs)

    landed = []
    rounds = [k for k in range(steps) if any((k + group * w) % steps == steps - 1 for w in kinds)]
    for k in range(steps):
        if k not in rounds:
            landed.append((k, 0, returned(k, chosen(k, lambda j: done[j]))))
    for k in rounds:
        block = chosen(k, lambda j: early if j == steps - 1 else done[j][late:])
        landed.append((k, late, returned(k, block)))
    for k in rounds:
        block = chosen(k, lambda j: begin if j == steps - 1 else done[j][:late])
        landed.append((k, 0, returned(k, block)))
    return assemble(landed, targets, rows, panel * group, kept)[:, None, :]


def assemble(landed, targets, rows, columns, kept):
    if kept % 128:
        output = jnp.zeros((rows, columns), BF16)
        for k, first, block in landed:
            output = lax.dynamic_update_slice(output, block, (first, targets[k]))
        return output
    count = len(landed)

    def body(targets, *refs):
        blocks, out, sems = refs[:count], refs[count], refs[count + 1]
        copies = []
        for i, (k, first, block) in enumerate(landed):
            column = pl.multiple_of(targets[k], 128)
            spot = out.at[pl.ds(first, block.shape[0]), pl.ds(column, kept)]
            copies.append(pltpu.make_async_copy(blocks[i], spot, sems.at[i]))
            copies[-1].start()
        for copy in copies:
            copy.wait()

    return pl.pallas_call(
        body,
        out_shape=jax.ShapeDtypeStruct((rows, columns), BF16),
        in_specs=[pl.BlockSpec(memory_space=pltpu.SMEM)] + [pl.BlockSpec(memory_space=pl.ANY)] * count,
        out_specs=pl.BlockSpec(memory_space=pl.ANY),
        scratch_shapes=[pltpu.SemaphoreType.DMA((count,))],
        compiler_params=pltpu.CompilerParams(vmem_limit_bytes=12 << 20),
        name="assemble",
    )(targets, *[block for _, _, block in landed])


def solution(mesh):
    placed = (
        P(("parts", "ctx"), "width"),
        P("width"),
        P(None, "width", "sub", "ctx"),
        P(None, None, "sub", "width"),
        P(None, "sub", "width"),
    )
    return jax.shard_map(
        shards,
        mesh=mesh,
        in_specs=placed,
        out_specs=P(("parts", "ctx"), "sub", "width"),
        check_vma=False,
    )
```

```python
import functools

import jax
import jax.numpy as jnp
import numpy as np
from jax import lax
from jax.experimental import pallas as pl
from jax.experimental.pallas import tpu as pltpu
from jax.sharding import PartitionSpec as P

EPSILON = 1e-05
HALO = 144
FFT = 256
STEP = 128
EXTRA = 8
BF16 = jnp.bfloat16
F32 = jnp.float32


def repeat(count, unrolled, body):
    if unrolled:
        for i in range(count):
            body(i)
    else:
        pl.loop(0, count)(body)


def at_multiple(value, multiple):
    return value if isinstance(value, int) else pl.multiple_of(value, multiple)


def split(matrix):
    high = np.asarray(matrix, np.float32).astype(jnp.bfloat16)
    low = (np.asarray(matrix, np.float32) - high.astype(np.float32)).astype(jnp.bfloat16)
    return high, low


def transforms():
    half = FFT // 2
    n = np.arange(FFT)
    k = np.arange(half)
    angle = 2.0 * np.pi * np.outer(k, n) / FFT
    real, imag = np.cos(angle), -np.sin(angle)
    imag[0] = np.cos(np.pi * n)
    forward = np.concatenate([real, imag], axis=0)
    weight = np.full((half,), 2.0)
    weight[0] = 1.0
    back_real = (weight[:, None] * np.cos(angle)).T / FFT
    back_imag = (-2.0 * np.sin(angle)).T / FFT
    back_imag[:, 0] = np.cos(np.pi * n) / FFT
    inverse = np.concatenate([back_real, back_imag], axis=1)[FFT - STEP :]
    return forward, inverse


def project(parts, rows, weight, places, column, kept):
    depth = parts[0].shape[1]
    streams = weight.shape[0]
    count = len(parts)

    narrow = weight.shape[2] == kept

    def body(places, *refs):
        blocks, weight, out = refs[:count], refs[count], refs[count + 1]
        columns = slice(None) if narrow else pl.ds(pl.multiple_of(places[column] * kept, kept), kept)

        def one(stream):
            total = None
            for offset, block in enumerate(blocks):
                row = pl.multiple_of(lax.rem(places[0] + offset, count) * depth, depth)
                term = jnp.dot(
                    block[:rows, :], weight[stream, pl.ds(row, depth), columns], preferred_element_type=F32
                )
                total = term if total is None else total + term
            out[stream] = total.astype(BF16)

        repeat(streams, rows < 256, one)

    whole = pl.BlockSpec(memory_space=pltpu.VMEM)
    return pl.pallas_call(
        body,
        out_shape=jax.ShapeDtypeStruct((streams, rows, kept), BF16),
        in_specs=[pl.BlockSpec(memory_space=pltpu.SMEM)] + [whole] * (count + 1),
        out_specs=whole,
        compiler_params=pltpu.CompilerParams(vmem_limit_bytes=12 << 20),
        cost_estimate=pl.CostEstimate(flops=1 << 20, bytes_accessed=1 << 16, transcendentals=0),
        name="project",
    )(places, *parts, pltpu.with_memory_space_constraint(weight, pltpu.VMEM))


def row_power(tokens):
    rows, features = tokens.shape
    tile = 128

    def body(block, out):
        values = block[...].astype(F32)
        total = jnp.sum(values * values, axis=1, keepdims=True)
        out[...] = jnp.broadcast_to(total, (tile, tile)).T[:EXTRA]

    return pl.pallas_call(
        body,
        out_shape=jax.ShapeDtypeStruct((EXTRA, rows), F32),
        grid=(rows // tile,),
        in_specs=[pl.BlockSpec((tile, features), lambda i: (i, 0))],
        out_specs=pl.BlockSpec((EXTRA, tile), lambda i: (0, i)),
        compiler_params=pltpu.CompilerParams(vmem_limit_bytes=12 << 20),
        cost_estimate=pl.CostEstimate(flops=1 << 20, bytes_accessed=1 << 16, transcendentals=0),
        name="power",
    )(tokens)


def filter_kernel(plan, terms, rows, flag, places, *refs):
    pieces = []
    for _ in plan:
        pieces.append(refs[:terms])
        refs = refs[terms:]
    near, far, short, spec_a, spec_b, spec_c, fh, fl, gh, gl, out, held, query, gated, spread = refs
    tile = 64
    kept = out.shape[1]
    extent = spread.shape[1]
    for which, scale in enumerate((near, far)):
        row = scale[0:1, :extent].astype(F32) + scale[1:2, :extent].astype(F32) + scale[2:3, :extent].astype(F32)
        for low in range(0, extent, 128):
            spread[which, low : low + 128, :] = jnp.broadcast_to(row[:, low : low + 128], (128, 128)).T
    at = 0
    for (first, count, scale, scale_first, masked), sources in zip(plan, pieces):
        for low in range(0, count, tile):
            size = min(tile, count - low)
            factor = spread[scale, scale_first + low : scale_first + low + size, :]
            if masked:
                factor = factor * places[flag].astype(F32)
            factor = jnp.concatenate([factor] * (kept // 128), axis=1) if kept % 128 == 0 else factor[:, :kept]
            for stream in range(3):
                total = sources[0][stream, first + low : first + low + size, :].astype(F32)
                for source in sources[1:]:
                    total = total + source[stream, first + low : first + low + size, :].astype(F32)
                value = (total * factor).astype(BF16).astype(F32)
                held[stream, at + low : at + low + size, :] = value
        at += count

    def short_filter(stream, row):
        window = held[stream, pl.ds(at_multiple(row - 8, 8), tile + 8), :]
        return sum(short[j, stream][None, :] * window[8 - j : 8 - j + tile] for j in range(3))

    lead = HALO - STEP

    def gate(i):
        low = at_multiple(i * tile, tile)
        value = short_filter(1, lead + low) * short_filter(2, lead + low)
        gated[pl.ds(low, tile), :] = value.astype(BF16)

    def ask(i):
        low = at_multiple(i * tile, tile)
        query[pl.ds(low, tile), :] = short_filter(0, HALO + low)

    half = FFT // 2

    def convolve(i):
        start = min(i * STEP, rows - STEP) if isinstance(i, int) else jnp.minimum(i * STEP, rows - STEP)
        start = at_multiple(start, tile)
        window = gated[pl.ds(start, FFT), :]
        spectrum = jnp.dot(fh[...], window, preferred_element_type=F32)
        spectrum = spectrum + jnp.dot(fl[...], window, preferred_element_type=F32)
        upper, lower = spectrum[:half], spectrum[half:]
        product = jnp.concatenate(
            [upper * spec_a[...] - lower * spec_b[...], upper * spec_b[...] + lower * spec_c[...]], axis=0
        )
        high = product.astype(BF16)
        rest = (product - high.astype(F32)).astype(BF16)
        result = jnp.dot(gh[...], high, preferred_element_type=F32)
        result = result + jnp.dot(gh[...], rest, preferred_element_type=F32)
        result = result + jnp.dot(gl[...], high, preferred_element_type=F32)
        out[pl.ds(start, STEP), :] = (result * query[pl.ds(start, STEP), :]).astype(BF16)

    unrolled = rows < 512
    repeat((STEP + rows) // tile, unrolled, gate)
    repeat(rows // tile, unrolled, ask)
    repeat(-(-rows // STEP), unrolled, convolve)


def filter_rows(plan, pieces, scales, flag, places, short, spectra, matrices, rows):
    terms = len(pieces[0])
    streams, _, kept = pieces[0][0].shape
    extent = scales[0].shape[1]
    arrays = [array for piece in pieces for array in piece]
    constants = [*scales, short, *spectra, *matrices]
    whole = pl.BlockSpec(memory_space=pltpu.VMEM)
    return pl.pallas_call(
        functools.partial(filter_kernel, plan, terms, rows, flag),
        out_shape=jax.ShapeDtypeStruct((rows, kept), BF16),
        in_specs=[pl.BlockSpec(memory_space=pltpu.SMEM)] + [whole] * (len(arrays) + len(constants)),
        out_specs=whole,
        scratch_shapes=[
            pltpu.VMEM((streams, HALO + rows, kept), F32),
            pltpu.VMEM((rows, kept), F32),
            pltpu.VMEM((STEP + rows, kept), BF16),
            pltpu.VMEM((2, extent, 128), F32),
        ],
        compiler_params=pltpu.CompilerParams(vmem_limit_bytes=12 << 20),
        cost_estimate=pl.CostEstimate(flops=1 << 20, bytes_accessed=1 << 16, transcendentals=0),
        name="filter",
    )(places, *arrays, *constants)


def shards(tokens, norm_gain, in_weight, short_taps, long_taps):
    steps, across, cores = (lax.axis_size(a) for a in ("ctx", "width", "sub"))
    z, x, sub = (lax.axis_index(a) for a in ("ctx", "width", "sub"))
    rows, features = tokens.shape
    panel = in_weight.shape[3]
    kept = panel // across
    group = steps // across
    owner = z // group
    depth = features // cores
    mid, small, late = rows // 2, 48, 192

    kinds = range(across)
    places = [sub] + [lax.rem(x + w, across) for w in kinds]
    flag_at = len(places)
    places += [jnp.where(z == k % steps, 0, 1) for k in range(steps)]
    starts = [lax.rem(sub + o, cores) * depth for o in range(cores)]
    part = lax.rem(x - owner + across, across)
    mine = [part == w for w in kinds]
    tap_first = [lax.rem(z, group) * panel + lax.rem(x + w, across) * kept for w in kinds]
    targets = []
    for k in range(steps):
        source = group * x + lax.rem(z + k, group)
        w = lax.rem((source - z - k + 2 * steps) // group, across)
        targets.append(lax.rem(source, group) * panel + lax.rem(x + w, across) * kept)
    places = jnp.stack(places).astype(jnp.int32)
    if kept % 128 == 0:
        targets = jnp.stack(targets).astype(jnp.int32)
    tokens, places, starts, mine, tap_first, targets = lax.optimization_barrier(
        (tokens, places, starts, mine, tap_first, targets)
    )

    def scaled_part(source, first, count, offset):
        block = lax.dynamic_slice(
            source, (jnp.int32(first), starts[offset]), (count, depth), allow_negative_indices=False
        ).astype(F32)
        gain = lax.dynamic_slice(norm_gain, (starts[offset],), (depth,), allow_negative_indices=False)
        return (block * gain[None, :]).astype(BF16)

    ring = [(i, (i + 1) % steps) for i in range(steps)]
    forward = lambda block: lax.ppermute(block, "ctx", ring)

    def sideways(block, w):
        return lax.ppermute(block, "width", [(i, (i + w) % across) for i in range(across)])

    def all_parts(block):
        swaps = [[((c + o) % cores, c) for c in range(cores)] for o in range(1, cores)]
        return [block] + [lax.ppermute(block, "sub", swap) for swap in swaps]

    weight = in_weight[:, :, 0, :]

    def partial(parts, count, w):
        if kept % 128:
            first = lax.rem(x + w, across) * kept
            narrow = lax.dynamic_slice_in_dim(weight, first, kept, 2)
            return project(parts, count, narrow, places, 1, kept)
        return project(parts, count, weight, places, 1 + w, kept)

    def partials(parts, count):
        sent = [partial(parts, count, w) for w in range(1, across)]
        received = [sideways(block, w + 1) for w, block in enumerate(sent)]
        kept_block = partial(parts, count, 0)
        return [kept_block] + sent, [kept_block] + received

    halves = [(mid, rows - mid), (0, mid)]
    last = [(mid, rows - mid), (small, mid - small), (0, small)]
    table, done, held = {}, {}, {}
    received, ready = [], set()
    waiting = []

    def multiply(key, parts, count):
        local, table[key] = partials(parts, count)
        held["local", key] = local
        received.append(key)
        return local

    first, count = halves[0]
    upper = scaled_part(tokens, first, count, 0)
    source, upper = lax.optimization_barrier((tokens, upper))
    own = [scaled_part(source, first, count, o) for o in range(1, cores)]
    first, count = halves[1]
    lowers = [scaled_part(source, first, count, o) for o in range(cores)]
    own, lowers = lax.optimization_barrier((own, lowers))
    first, count = halves[0]
    local = multiply((0, first), [upper] + own, count)
    source, short_taps, long_taps, _ = lax.optimization_barrier((source, short_taps, long_taps, local[1:]))

    power = row_power(source)
    whole_power = power
    for w in range(1, across):
        whole_power = whole_power + sideways(power, w)
    scale = lax.rsqrt(whole_power / (features * across) + EPSILON)
    terms = [lax.reduce_precision(scale, 8, 7)]
    terms.append(lax.reduce_precision(scale - terms[0], 8, 7))
    terms.append(scale - terms[0] - terms[1])
    line = lax.broadcasted_iota(jnp.int32, scale.shape, 0)
    extra = jnp.where(line == 0, terms[0], jnp.where(line == 1, terms[1], jnp.where(line == 2, terms[2], 0.0)))
    extra = jnp.pad(extra.astype(BF16), ((0, 0), (0, depth - rows)))
    first, count = halves[1]
    lower = jnp.concatenate([lowers[0], extra], axis=0)
    scales = [extra[:, :rows]]
    waiting.append(((0, first), [lower] + lowers[1:], count))

    def taps_of(taps):
        cut = lambda w: lax.dynamic_slice_in_dim(taps, tap_first[w], kept, taps.ndim - 1, allow_negative_indices=False)
        result = cut(0)
        for w in range(1, across):
            other = sideways(cut(w), w)
            result = jnp.where(mine[w], other, result)
        return result

    short = taps_of(short_taps[:, :, 0, :])
    long = taps_of(long_taps[:, 0, :])
    forward_dft, inverse_dft = transforms()
    spectrum = jnp.dot(
        jnp.asarray(forward_dft[:, : long.shape[0]], F32), long, precision=lax.Precision.HIGHEST
    )
    real, imag = spectrum[: FFT // 2], spectrum[FFT // 2 :]
    first_row = (jnp.arange(FFT // 2) == 0)[:, None]
    spectra = [real, jnp.where(first_row, 0.0, imag), jnp.where(first_row, imag, real)]
    matrices = [jnp.asarray(m) for pair in (split(forward_dft), split(inverse_dft)) for m in pair]

    def unit(step, plan, pieces, count):
        near_far = (scales[step], scales[(step + 1) % steps])
        return filter_rows(plan, pieces, near_far, flag_at + step, places, short, spectra, matrices, count)

    tail = rows - mid
    before = (tail - HALO, HALO, 1, rows - HALO, True)

    def whole_unit(step):
        plan = (before, (0, mid, 0, 0, False), (0, tail, 0, mid, False))
        return unit(step, plan, [table[step + 1, mid], table[step, 0], table[step, mid]], rows)

    held["filters", 0] = (short, spectra)

    def arrived(block, final=False):
        coming = [key for key in (received if final else received[:-1]) if key not in ready]
        names = list(held)
        pack = (block, [held[n] for n in names], [table[key] for key in coming])
        block, kept_back, blocks = lax.optimization_barrier(pack)
        for key, value in zip(coming, blocks):
            table[key] = value
            ready.add(key)
        for name, value in zip(names, kept_back):
            if name[0] == "unit":
                done[name[1]] = value
        held.clear()
        return block

    def filter_ready():
        for step in range(steps - 1):
            if step not in done and {(step + 1, mid), (step, 0), (step, mid)} <= ready:
                done[step] = whole_unit(step)
                held["unit", step] = done[step]

    moving = [upper, lower]
    for step in range(1, steps):
        if step < steps - 1:
            spans = halves
            moving = [forward(block) for block in moving]
        else:
            spans = last
            upper, lower = moving
            moving = [forward(upper), forward(lower[small:]), forward(lower[:small])]
        for i, (first, count) in enumerate(spans):
            moving[i] = arrived(moving[i], step == steps - 1 and i <= 1)
            if i == 1:
                scales.append(moving[1][-EXTRA:, :rows])
            if step == 1 and i == 0:
                (key, parts, number), = waiting
                moving[i], parts = lax.optimization_barrier((moving[i], parts))
                waiting = [(key, parts, number)]
            waiting.append(((step, first), all_parts(moving[i]), count))
            if len(waiting) > 1:
                multiply(*waiting.pop(0))
            filter_ready()
    crossing = [[sideways(partial(parts, count, w), w) for w in range(1, across)] for _, parts, count in waiting]
    for step in range(steps - 1):
        if step not in done:
            done[step] = whole_unit(step)
    blocks, done = lax.optimization_barrier(([parts for _, parts, _ in waiting], done))
    for (key, _, count), parts, terms in zip(waiting, blocks, crossing):
        table[key] = [partial(parts, count, 0)] + terms
    step = steps - 1
    early = unit(
        step,
        ((late - HALO - small, mid - (late - HALO), 0, late - HALO, False), (0, tail, 0, mid, False)),
        [table[step, small], table[step, mid]],
        rows - late,
    )
    begin = unit(
        step,
        (before, (0, small, 0, 0, False), (0, late - small, 0, small, False)),
        [table[0, mid], table[step, 0], table[step, small]],
        late,
    )

    def chosen(k, cut):
        options = [cut((k + group * w) % steps) for w in kinds]
        result = options[0]
        for w in range(1, across):
            result = jnp.where(mine[w], options[w], result)
        return result

    def returned(k, block):
        pairs = []
        for c in range(steps):
            for v in kinds:
                w = (v - c // group) % across
                target = (c - k - group * w) % steps
                pairs.append((c * across + v, target * across + c // group))
        return lax.ppermute(block, ("ctx", "width"), pairs)

    landed = []
    rounds = [k for k in range(steps) if any((k + group * w) % steps == steps - 1 for w in kinds)]
    for k in range(steps):
        if k not in rounds:
            landed.append((k, 0, returned(k, chosen(k, lambda j: done[j]))))
    for k in rounds:
        block = chosen(k, lambda j: early if j == steps - 1 else done[j][late:])
        landed.append((k, late, returned(k, block)))
    for k in rounds:
        block = chosen(k, lambda j: begin if j == steps - 1 else done[j][:late])
        landed.append((k, 0, returned(k, block)))
    return assemble(landed, targets, rows, panel * group, kept)[:, None, :]


def assemble(landed, targets, rows, columns, kept):
    if kept % 128:
        output = jnp.zeros((rows, columns), BF16)
        for k, first, block in landed:
            output = lax.dynamic_update_slice(output, block, (first, targets[k]))
        return output
    count = len(landed)

    def body(targets, *refs):
        blocks, out, sems = refs[:count], refs[count], refs[count + 1]
        copies = []
        for i, (k, first, block) in enumerate(landed):
            column = pl.multiple_of(targets[k], 128)
            spot = out.at[pl.ds(first, block.shape[0]), pl.ds(column, kept)]
            copies.append(pltpu.make_async_copy(blocks[i], spot, sems.at[i]))
            copies[-1].start()
        for copy in copies:
            copy.wait()

    return pl.pallas_call(
        body,
        out_shape=jax.ShapeDtypeStruct((rows, columns), BF16),
        in_specs=[pl.BlockSpec(memory_space=pltpu.SMEM)] + [pl.BlockSpec(memory_space=pl.ANY)] * count,
        out_specs=pl.BlockSpec(memory_space=pl.ANY),
        scratch_shapes=[pltpu.SemaphoreType.DMA((count,))],
        compiler_params=pltpu.CompilerParams(vmem_limit_bytes=12 << 20),
        name="assemble",
    )(targets, *[block for _, _, block in landed])


def solution(mesh):
    placed = (
        P(("parts", "ctx"), "width"),
        P("width"),
        P(None, "width", "sub", "ctx"),
        P(None, None, "sub", "width"),
        P(None, "sub", "width"),
    )
    return jax.shard_map(
        shards,
        mesh=mesh,
        in_specs=placed,
        out_specs=P(("parts", "ctx"), "sub", "width"),
        check_vma=False,
    )
```

```python
import functools

import jax
import jax.numpy as jnp
import numpy as np
from jax import lax
from jax.experimental import pallas as pl
from jax.experimental.pallas import tpu as pltpu
from jax.sharding import PartitionSpec as P

EPSILON = 1e-05
HALO = 144
FFT = 256
STEP = 128
EXTRA = 8
BF16 = jnp.bfloat16
F32 = jnp.float32


def repeat(count, unrolled, body):
    if unrolled:
        for i in range(count):
            body(i)
    else:
        pl.loop(0, count)(body)


def at_multiple(value, multiple):
    return value if isinstance(value, int) else pl.multiple_of(value, multiple)


def split(matrix):
    high = np.asarray(matrix, np.float32).astype(jnp.bfloat16)
    low = (np.asarray(matrix, np.float32) - high.astype(np.float32)).astype(jnp.bfloat16)
    return high, low


def transforms():
    half = FFT // 2
    n = np.arange(FFT)
    k = np.arange(half)
    angle = 2.0 * np.pi * np.outer(k, n) / FFT
    real, imag = np.cos(angle), -np.sin(angle)
    imag[0] = np.cos(np.pi * n)
    forward = np.concatenate([real, imag], axis=0)
    weight = np.full((half,), 2.0)
    weight[0] = 1.0
    back_real = (weight[:, None] * np.cos(angle)).T / FFT
    back_imag = (-2.0 * np.sin(angle)).T / FFT
    back_imag[:, 0] = np.cos(np.pi * n) / FFT
    inverse = np.concatenate([back_real, back_imag], axis=1)[FFT - STEP :]
    return forward, inverse


def project(parts, rows, weight, places, column, kept):
    depth = parts[0].shape[1]
    streams = weight.shape[0]
    count = len(parts)

    narrow = weight.shape[2] == kept

    def body(places, *refs):
        blocks, weight, out = refs[:count], refs[count], refs[count + 1]
        columns = slice(None) if narrow else pl.ds(pl.multiple_of(places[column] * kept, kept), kept)

        def one(stream):
            total = None
            for offset, block in enumerate(blocks):
                row = pl.multiple_of(lax.rem(places[0] + offset, count) * depth, depth)
                term = jnp.dot(
                    block[:rows, :], weight[stream, pl.ds(row, depth), columns], preferred_element_type=F32
                )
                total = term if total is None else total + term
            out[stream] = total.astype(BF16)

        repeat(streams, rows < 256, one)

    whole = pl.BlockSpec(memory_space=pltpu.VMEM)
    return pl.pallas_call(
        body,
        out_shape=jax.ShapeDtypeStruct((streams, rows, kept), BF16),
        in_specs=[pl.BlockSpec(memory_space=pltpu.SMEM)] + [whole] * (count + 1),
        out_specs=whole,
        compiler_params=pltpu.CompilerParams(vmem_limit_bytes=12 << 20),
        cost_estimate=pl.CostEstimate(flops=1 << 20, bytes_accessed=1 << 16, transcendentals=0),
        name="project",
    )(places, *parts, pltpu.with_memory_space_constraint(weight, pltpu.VMEM))


def row_power(tokens):
    rows, features = tokens.shape
    tile = 128

    def body(block, out):
        values = block[...].astype(F32)
        total = jnp.sum(values * values, axis=1, keepdims=True)
        out[...] = jnp.broadcast_to(total, (tile, tile)).T[:EXTRA]

    return pl.pallas_call(
        body,
        out_shape=jax.ShapeDtypeStruct((EXTRA, rows), F32),
        grid=(rows // tile,),
        in_specs=[pl.BlockSpec((tile, features), lambda i: (i, 0))],
        out_specs=pl.BlockSpec((EXTRA, tile), lambda i: (0, i)),
        compiler_params=pltpu.CompilerParams(vmem_limit_bytes=12 << 20),
        cost_estimate=pl.CostEstimate(flops=1 << 20, bytes_accessed=1 << 16, transcendentals=0),
        name="power",
    )(tokens)


def filter_kernel(plan, terms, rows, flag, places, *refs):
    pieces = []
    for _ in plan:
        pieces.append(refs[:terms])
        refs = refs[terms:]
    near, far, short, spec_a, spec_b, spec_c, fh, fl, gh, gl, out, held, query, gated, spread = refs
    tile = 64
    kept = out.shape[1]
    extent = spread.shape[1]
    for which, scale in enumerate((near, far)):
        row = scale[0:1, :extent].astype(F32) + scale[1:2, :extent].astype(F32) + scale[2:3, :extent].astype(F32)
        for low in range(0, extent, 128):
            spread[which, low : low + 128, :] = jnp.broadcast_to(row[:, low : low + 128], (128, 128)).T
    at = 0
    for (first, count, scale, scale_first, masked), sources in zip(plan, pieces):
        for low in range(0, count, tile):
            size = min(tile, count - low)
            factor = spread[scale, scale_first + low : scale_first + low + size, :]
            if masked:
                factor = factor * places[flag].astype(F32)
            factor = jnp.concatenate([factor] * (kept // 128), axis=1) if kept % 128 == 0 else factor[:, :kept]
            for stream in range(3):
                total = sources[0][stream, first + low : first + low + size, :].astype(F32)
                for source in sources[1:]:
                    total = total + source[stream, first + low : first + low + size, :].astype(F32)
                value = (total * factor).astype(BF16).astype(F32)
                held[stream, at + low : at + low + size, :] = value
        at += count

    def short_filter(stream, row):
        window = held[stream, pl.ds(at_multiple(row - 8, 8), tile + 8), :]
        return sum(short[j, stream][None, :] * window[8 - j : 8 - j + tile] for j in range(3))

    lead = HALO - STEP

    def gate(i):
        low = at_multiple(i * tile, tile)
        value = short_filter(1, lead + low) * short_filter(2, lead + low)
        gated[pl.ds(low, tile), :] = value.astype(BF16)

    def ask(i):
        low = at_multiple(i * tile, tile)
        query[pl.ds(low, tile), :] = short_filter(0, HALO + low)

    half = FFT // 2

    def convolve(i):
        start = min(i * STEP, rows - STEP) if isinstance(i, int) else jnp.minimum(i * STEP, rows - STEP)
        start = at_multiple(start, tile)
        window = gated[pl.ds(start, FFT), :]
        spectrum = jnp.dot(fh[...], window, preferred_element_type=F32)
        spectrum = spectrum + jnp.dot(fl[...], window, preferred_element_type=F32)
        upper, lower = spectrum[:half], spectrum[half:]
        product = jnp.concatenate(
            [upper * spec_a[...] - lower * spec_b[...], upper * spec_b[...] + lower * spec_c[...]], axis=0
        )
        high = product.astype(BF16)
        rest = (product - high.astype(F32)).astype(BF16)
        result = jnp.dot(gh[...], high, preferred_element_type=F32)
        result = result + jnp.dot(gh[...], rest, preferred_element_type=F32)
        result = result + jnp.dot(gl[...], high, preferred_element_type=F32)
        out[pl.ds(start, STEP), :] = (result * query[pl.ds(start, STEP), :]).astype(BF16)

    unrolled = True
    repeat((STEP + rows) // tile, unrolled, gate)
    repeat(rows // tile, unrolled, ask)
    repeat(-(-rows // STEP), unrolled, convolve)


def filter_rows(plan, pieces, scales, flag, places, short, spectra, matrices, rows):
    terms = len(pieces[0])
    streams, _, kept = pieces[0][0].shape
    extent = scales[0].shape[1]
    arrays = [array for piece in pieces for array in piece]
    constants = [*scales, short, *spectra, *matrices]
    whole = pl.BlockSpec(memory_space=pltpu.VMEM)
    return pl.pallas_call(
        functools.partial(filter_kernel, plan, terms, rows, flag),
        out_shape=jax.ShapeDtypeStruct((rows, kept), BF16),
        in_specs=[pl.BlockSpec(memory_space=pltpu.SMEM)] + [whole] * (len(arrays) + len(constants)),
        out_specs=whole,
        scratch_shapes=[
            pltpu.VMEM((streams, HALO + rows, kept), F32),
            pltpu.VMEM((rows, kept), F32),
            pltpu.VMEM((STEP + rows, kept), BF16),
            pltpu.VMEM((2, extent, 128), F32),
        ],
        compiler_params=pltpu.CompilerParams(vmem_limit_bytes=12 << 20),
        cost_estimate=pl.CostEstimate(flops=1 << 20, bytes_accessed=1 << 16, transcendentals=0),
        name="filter",
    )(places, *arrays, *constants)


def shards(tokens, norm_gain, in_weight, short_taps, long_taps):
    steps, across, cores = (lax.axis_size(a) for a in ("ctx", "width", "sub"))
    z, x, sub = (lax.axis_index(a) for a in ("ctx", "width", "sub"))
    rows, features = tokens.shape
    panel = in_weight.shape[3]
    kept = panel // across
    group = steps // across
    owner = z // group
    depth = features // cores
    mid, small, late = rows // 2, 48, 192

    kinds = range(across)
    places = [sub] + [lax.rem(x + w, across) for w in kinds]
    flag_at = len(places)
    places += [jnp.where(z == k % steps, 0, 1) for k in range(steps)]
    starts = [lax.rem(sub + o, cores) * depth for o in range(cores)]
    part = lax.rem(x - owner + across, across)
    mine = [part == w for w in kinds]
    tap_first = [lax.rem(z, group) * panel + lax.rem(x + w, across) * kept for w in kinds]
    targets = []
    for k in range(steps):
        source = group * x + lax.rem(z + k, group)
        w = lax.rem((source - z - k + 2 * steps) // group, across)
        targets.append(lax.rem(source, group) * panel + lax.rem(x + w, across) * kept)
    places = jnp.stack(places).astype(jnp.int32)
    if kept % 128 == 0:
        targets = jnp.stack(targets).astype(jnp.int32)
    tokens, places, starts, mine, tap_first, targets = lax.optimization_barrier(
        (tokens, places, starts, mine, tap_first, targets)
    )

    def scaled_part(source, first, count, offset):
        block = lax.dynamic_slice(
            source, (jnp.int32(first), starts[offset]), (count, depth), allow_negative_indices=False
        ).astype(F32)
        gain = lax.dynamic_slice(norm_gain, (starts[offset],), (depth,), allow_negative_indices=False)
        return (block * gain[None, :]).astype(BF16)

    ring = [(i, (i + 1) % steps) for i in range(steps)]
    forward = lambda block: lax.ppermute(block, "ctx", ring)

    def sideways(block, w):
        return lax.ppermute(block, "width", [(i, (i + w) % across) for i in range(across)])

    def all_parts(block):
        swaps = [[((c + o) % cores, c) for c in range(cores)] for o in range(1, cores)]
        return [block] + [lax.ppermute(block, "sub", swap) for swap in swaps]

    weight = in_weight[:, :, 0, :]

    def partial(parts, count, w):
        if kept % 128:
            first = lax.rem(x + w, across) * kept
            narrow = lax.dynamic_slice_in_dim(weight, first, kept, 2)
            return project(parts, count, narrow, places, 1, kept)
        return project(parts, count, weight, places, 1 + w, kept)

    def partials(parts, count):
        sent = [partial(parts, count, w) for w in range(1, across)]
        received = [sideways(block, w + 1) for w, block in enumerate(sent)]
        kept_block = partial(parts, count, 0)
        return [kept_block] + sent, [kept_block] + received

    halves = [(mid, rows - mid), (0, mid)]
    last = [(mid, rows - mid), (small, mid - small), (0, small)]
    table, done, held = {}, {}, {}
    received, ready = [], set()
    waiting = []

    def multiply(key, parts, count):
        local, table[key] = partials(parts, count)
        held["local", key] = local
        received.append(key)
        return local

    first, count = halves[0]
    upper = scaled_part(tokens, first, count, 0)
    source, upper = lax.optimization_barrier((tokens, upper))
    own = [scaled_part(source, first, count, o) for o in range(1, cores)]
    first, count = halves[1]
    lowers = [scaled_part(source, first, count, o) for o in range(cores)]
    own, lowers = lax.optimization_barrier((own, lowers))
    first, count = halves[0]
    local = multiply((0, first), [upper] + own, count)
    source, short_taps, long_taps, _ = lax.optimization_barrier((source, short_taps, long_taps, local[1:]))

    power = row_power(source)
    whole_power = power
    for w in range(1, across):
        whole_power = whole_power + sideways(power, w)
    scale = lax.rsqrt(whole_power / (features * across) + EPSILON)
    terms = [lax.reduce_precision(scale, 8, 7)]
    terms.append(lax.reduce_precision(scale - terms[0], 8, 7))
    terms.append(scale - terms[0] - terms[1])
    line = lax.broadcasted_iota(jnp.int32, scale.shape, 0)
    extra = jnp.where(line == 0, terms[0], jnp.where(line == 1, terms[1], jnp.where(line == 2, terms[2], 0.0)))
    extra = jnp.pad(extra.astype(BF16), ((0, 0), (0, depth - rows)))
    first, count = halves[1]
    lower = jnp.concatenate([lowers[0], extra], axis=0)
    scales = [extra[:, :rows]]
    waiting.append(((0, first), [lower] + lowers[1:], count))

    def taps_of(taps):
        cut = lambda w: lax.dynamic_slice_in_dim(taps, tap_first[w], kept, taps.ndim - 1, allow_negative_indices=False)
        result = cut(0)
        for w in range(1, across):
            other = sideways(cut(w), w)
            result = jnp.where(mine[w], other, result)
        return result

    short = taps_of(short_taps[:, :, 0, :])
    long = taps_of(long_taps[:, 0, :])
    forward_dft, inverse_dft = transforms()
    spectrum = jnp.dot(
        jnp.asarray(forward_dft[:, : long.shape[0]], F32), long, precision=lax.Precision.HIGHEST
    )
    real, imag = spectrum[: FFT // 2], spectrum[FFT // 2 :]
    first_row = (jnp.arange(FFT // 2) == 0)[:, None]
    spectra = [real, jnp.where(first_row, 0.0, imag), jnp.where(first_row, imag, real)]
    matrices = [jnp.asarray(m) for pair in (split(forward_dft), split(inverse_dft)) for m in pair]

    def unit(step, plan, pieces, count):
        near_far = (scales[step], scales[(step + 1) % steps])
        return filter_rows(plan, pieces, near_far, flag_at + step, places, short, spectra, matrices, count)

    tail = rows - mid
    before = (tail - HALO, HALO, 1, rows - HALO, True)

    def whole_unit(step):
        plan = (before, (0, mid, 0, 0, False), (0, tail, 0, mid, False))
        return unit(step, plan, [table[step + 1, mid], table[step, 0], table[step, mid]], rows)

    held["filters", 0] = (short, spectra)

    def arrived(block, final=False):
        coming = [key for key in (received if final else received[:-1]) if key not in ready]
        names = list(held)
        pack = (block, [held[n] for n in names], [table[key] for key in coming])
        block, kept_back, blocks = lax.optimization_barrier(pack)
        for key, value in zip(coming, blocks):
            table[key] = value
            ready.add(key)
        for name, value in zip(names, kept_back):
            if name[0] == "unit":
                done[name[1]] = value
        held.clear()
        return block

    def filter_ready():
        for step in range(steps - 1):
            if step not in done and {(step + 1, mid), (step, 0), (step, mid)} <= ready:
                done[step] = whole_unit(step)
                held["unit", step] = done[step]

    moving = [upper, lower]
    for step in range(1, steps):
        if step < steps - 1:
            spans = halves
            moving = [forward(block) for block in moving]
        else:
            spans = last
            upper, lower = moving
            moving = [forward(upper), forward(lower[small:]), forward(lower[:small])]
        for i, (first, count) in enumerate(spans):
            moving[i] = arrived(moving[i], step == steps - 1 and i <= 1)
            if i == 1:
                scales.append(moving[1][-EXTRA:, :rows])
            if step == 1 and i == 0:
                (key, parts, number), = waiting
                moving[i], parts = lax.optimization_barrier((moving[i], parts))
                waiting = [(key, parts, number)]
            waiting.append(((step, first), all_parts(moving[i]), count))
            if len(waiting) > 1:
                multiply(*waiting.pop(0))
            filter_ready()
    crossing = [[sideways(partial(parts, count, w), w) for w in range(1, across)] for _, parts, count in waiting]
    for step in range(steps - 1):
        if step not in done:
            done[step] = whole_unit(step)
    blocks, done = lax.optimization_barrier(([parts for _, parts, _ in waiting], done))
    for (key, _, count), parts, terms in zip(waiting, blocks, crossing):
        table[key] = [partial(parts, count, 0)] + terms
    step = steps - 1
    early = unit(
        step,
        ((late - HALO - small, mid - (late - HALO), 0, late - HALO, False), (0, tail, 0, mid, False)),
        [table[step, small], table[step, mid]],
        rows - late,
    )
    begin = unit(
        step,
        (before, (0, small, 0, 0, False), (0, late - small, 0, small, False)),
        [table[0, mid], table[step, 0], table[step, small]],
        late,
    )

    def chosen(k, cut):
        options = [cut((k + group * w) % steps) for w in kinds]
        result = options[0]
        for w in range(1, across):
            result = jnp.where(mine[w], options[w], result)
        return result

    def returned(k, block):
        pairs = []
        for c in range(steps):
            for v in kinds:
                w = (v - c // group) % across
                target = (c - k - group * w) % steps
                pairs.append((c * across + v, target * across + c // group))
        return lax.ppermute(block, ("ctx", "width"), pairs)

    landed = []
    rounds = [k for k in range(steps) if any((k + group * w) % steps == steps - 1 for w in kinds)]
    for k in range(steps):
        if k not in rounds:
            landed.append((k, 0, returned(k, chosen(k, lambda j: done[j]))))
    for k in rounds:
        block = chosen(k, lambda j: early if j == steps - 1 else done[j][late:])
        landed.append((k, late, returned(k, block)))
    for k in rounds:
        block = chosen(k, lambda j: begin if j == steps - 1 else done[j][:late])
        landed.append((k, 0, returned(k, block)))
    return assemble(landed, targets, rows, panel * group, kept)[:, None, :]


def assemble(landed, targets, rows, columns, kept):
    if kept % 128:
        output = jnp.zeros((rows, columns), BF16)
        for k, first, block in landed:
            output = lax.dynamic_update_slice(output, block, (first, targets[k]))
        return output
    count = len(landed)

    def body(targets, *refs):
        blocks, out, sems = refs[:count], refs[count], refs[count + 1]
        copies = []
        for i, (k, first, block) in enumerate(landed):
            column = pl.multiple_of(targets[k], 128)
            spot = out.at[pl.ds(first, block.shape[0]), pl.ds(column, kept)]
            copies.append(pltpu.make_async_copy(blocks[i], spot, sems.at[i]))
            copies[-1].start()
        for copy in copies:
            copy.wait()

    return pl.pallas_call(
        body,
        out_shape=jax.ShapeDtypeStruct((rows, columns), BF16),
        in_specs=[pl.BlockSpec(memory_space=pltpu.SMEM)] + [pl.BlockSpec(memory_space=pl.ANY)] * count,
        out_specs=pl.BlockSpec(memory_space=pl.ANY),
        scratch_shapes=[pltpu.SemaphoreType.DMA((count,))],
        compiler_params=pltpu.CompilerParams(vmem_limit_bytes=12 << 20),
        name="assemble",
    )(targets, *[block for _, _, block in landed])


def solution(mesh):
    placed = (
        P(("parts", "ctx"), "width"),
        P("width"),
        P(None, "width", "sub", "ctx"),
        P(None, None, "sub", "width"),
        P(None, "sub", "width"),
    )
    return jax.shard_map(
        shards,
        mesh=mesh,
        in_specs=placed,
        out_specs=P(("parts", "ctx"), "sub", "width"),
        check_vma=False,
    )
```
